32 devices in a mesh: groups: 2 (over y), ctx: 8 (over z, x), head: 2 (over core).
Axes of the slice: x: 2, y: 2, z: 4, core: 2. Of those that a mesh axis runs over, the one named last changes fastest.
Arguments:
- queries: bfloat16 [128, 64, 128], P(('groups', 'ctx'), 'head'), parts along dimension 0, may hold values from -600 to 600
- key_cache: bfloat16 [131072, 4, 128], P(('groups', 'ctx'), 'head'), parts along dimension 0, may hold values from -6 to 6
- value_cache: bfloat16 [131072, 4, 128], P(('groups', 'ctx'), 'head'), parts along dimension 0, may hold values from -6 to 6
- key_scale: float32 [1024, 4], P('groups', 'head'), parts along dimension 0, may hold values from 0.7 to 1.4
- value_scale: float32 [1024, 4], P('groups', 'head'), parts along dimension 0, may hold values from 0.5 to 2
- visits: int32 [12, 8], P('groups'), parts along dimension 0, may hold values from 0 to 7, as said below
- key_lists: int32 [16, 6, 32], P('groups'), parts along dimension 0, may hold values from 4 to 63, as said below
- out_weight: bfloat16 [8192, 16384], P('head', 'ctx'), may hold values from -0.0625 to 0.0625
Outputs:
- projected: bfloat16 [128, 16384], P(('groups', 'head'), 'ctx'), parts along dimension 0
The draws below stay inside these ranges and needn't reach their ends.
There are 2 independent parts, one for each index of `groups`. The reference program is written for one: setup_inputs(seed, part) draws one part's arguments, and reference() takes and returns one part's arrays. A program takes and returns all parts, laid end to end along the dimension named above; an argument that names none is the same for every part. Nothing has to cross between parts.
Inputs may be any that keep to these rules, and one draw needn't show every extreme that they name: For each stop s there is a mask m_s with visits[s, b] = b XOR m_s for every query block b; the 6 masks differ, so every row is a permutation of the context shards and the 6 shards that serve one query block all differ. `key_lists`: the 32 entries of one query block and stop are distinct local block numbers of the serving shard, never among its first 4.
All inputs are finite; a program needn't handle non-finite values.
Results may differ from the reference program's by a relative error of at most 0.0056.
Values may be sent and summed in bfloat16 or wider, within the bound.
A program may use at most 128 MiB of HBM per device.

```python
import math
import jax
import jax.numpy as jnp
from jax import lax

D = 16384
HEADS = 64
KV_HEADS = 4
HEAD_DIM = 128
BLOCK = 128
BLOCKS_DEV = 64
LIST = 32
STOPS = 6
GLOBAL = 4
QBLK = 8
CONTEXT = 65536
QUERIES = 64


def drawn_keys(key):
    stored = jnp.clip(jax.random.normal(jax.random.fold_in(key, 11), (CONTEXT, KV_HEADS, HEAD_DIM), jnp.float32), -6.0, 6.0)
    return stored


def draw_key_cache(key, part):
    return drawn_keys(key).astype(jnp.bfloat16)


def draw_queries(key, part):
    base_rows = jnp.clip(3.0 * jax.random.normal(jax.random.fold_in(key, 12), (QUERIES, HEADS, HEAD_DIM), jnp.float32), -18.0, 18.0)
    return base_rows.astype(jnp.bfloat16)


def draw_visits(key, part):
    shards = QUERIES // QBLK
    masks = jax.random.permutation(jax.random.fold_in(key, 31), shards)[:STOPS].astype(jnp.int32)
    block_ids = jnp.arange(shards, dtype=jnp.int32)
    return jnp.bitwise_xor(block_ids[None, :], masks[:, None]).astype(jnp.int32)


def draw_key_lists(key, part):
    shards = QUERIES // QBLK
    usable = BLOCKS_DEV - GLOBAL
    subkeys = jax.random.split(jax.random.fold_in(key, 21), shards * STOPS)
    orders = jax.vmap(lambda sub_key: jax.random.permutation(sub_key, usable))(subkeys)
    return (orders[:, :LIST] + GLOBAL).reshape(shards, STOPS, LIST).astype(jnp.int32)


def block_levels(key, dims, cuts, low, top_value):
    gain = 1.0
    for dim, shards_of in cuts:
        heights = jax.random.uniform(jax.random.fold_in(jax.random.fold_in(key, 6), dim), (shards_of,), jnp.float32, low / len(cuts), top_value / len(cuts))
        gain = gain * jnp.repeat(jnp.exp(heights), dims[dim] // shards_of).reshape((-1,) + (1,) * (len(dims) - 1 - dim))
    return gain


def bell_draw(rng, shape, scale, bound, cuts=(), kind=jnp.bfloat16):
    array = jax.random.normal(rng, shape, jnp.float32) * scale
    if len(cuts) > 0:
        array = block_levels(rng, shape, cuts, -0.22, 0.18) * array
    return jnp.clip(array, min=-bound, max=bound).astype(kind)


def setup_inputs(seed: int = 0, part: int = 0) -> dict:
    key_of = jax.random.split(jax.random.key(seed), 9)
    part_splits = jax.random.split(jax.random.fold_in(key_of[8], part), 9)
    return {
        "queries": draw_queries(jax.random.fold_in(jax.random.fold_in(key_of[8], part), 71), part),
        "key_cache": draw_key_cache(jax.random.fold_in(jax.random.fold_in(key_of[8], part), 71), part),
        "value_cache": bell_draw(part_splits[2], (CONTEXT, KV_HEADS, HEAD_DIM), 1.0, 6.0, ((0, 8), (1, 2))),
        "key_scale": jnp.clip(jnp.exp(math.log(1.4) - 0.6931472 * jax.random.uniform(part_splits[3], (CONTEXT // BLOCK, KV_HEADS), jnp.float32) ** block_levels(part_splits[3], (CONTEXT // BLOCK, KV_HEADS), ((1, 2),), -0.2, 0.2)), 0.7, 1.4),
        "value_scale": jnp.clip(jnp.exp(math.log(2.0) - 1.3862944 * jax.random.uniform(part_splits[4], (CONTEXT // BLOCK, KV_HEADS), jnp.float32) ** block_levels(part_splits[4], (CONTEXT // BLOCK, KV_HEADS), ((1, 2),), -0.2, 0.2)), 0.5, 2.0),
        "visits": draw_visits(jax.random.fold_in(jax.random.fold_in(key_of[8], part), 71), part),
        "key_lists": draw_key_lists(jax.random.fold_in(jax.random.fold_in(key_of[8], part), 71), part),
        "out_weight": bell_draw(key_of[7], (HEADS * HEAD_DIM, D), (HEADS * HEAD_DIM) ** -0.5, 0.0625, ((0, 2), (1, 8))),
    }


def attend(query_rows, key_rows, value_rows, key_factor, value_factor):
    num_rows = query_rows.shape[0]
    grouped = query_rows.reshape(num_rows, KV_HEADS, HEADS // KV_HEADS, HEAD_DIM).astype(jnp.float32)
    scores = jnp.einsum("qgjd,kgd->qgjk", grouped, key_rows.astype(jnp.float32))
    scores = scores * (key_factor.T[None, :, None, :] * HEAD_DIM ** -0.5)
    row_peak = jnp.max(scores, axis=-1)
    exponent = jnp.exp(scores - row_peak[..., None])
    totals = jnp.sum(exponent, axis=-1)
    weights = (exponent * value_factor.T[None, :, None, :]).astype(jnp.bfloat16)
    weighted = jnp.einsum("qgjk,kgd->qgjd", weights.astype(jnp.float32), value_rows.astype(jnp.float32))
    return row_peak, totals, weighted


def reference(queries, key_cache, value_cache, key_scale, value_scale, visits, key_lists, out_weight):
    shards = QUERIES // QBLK
    glob_keys = key_cache[:GLOBAL * BLOCK]
    glob_values = value_cache[:GLOBAL * BLOCK]
    glob_kfactor = jnp.repeat(key_scale[:GLOBAL], BLOCK, axis=0)
    glob_vfactor = jnp.repeat(value_scale[:GLOBAL], BLOCK, axis=0)
    offsets = jnp.arange(BLOCK, dtype=jnp.int32)

    def one_block(block_index):
        query_rows = lax.dynamic_slice_in_dim(queries, block_index * QBLK, QBLK, 0)
        visit_parts = [attend(query_rows, glob_keys, glob_values, glob_kfactor, glob_vfactor)]
        for stop_index in range(STOPS):
            owner = visits[stop_index, block_index]
            numbers = (owner * BLOCKS_DEV + key_lists[block_index, stop_index]).astype(jnp.int32)
            positions = (numbers[:, None] * BLOCK + offsets[None, :]).reshape(-1)
            key_factor = jnp.repeat(key_scale[numbers], BLOCK, axis=0)
            value_factor = jnp.repeat(value_scale[numbers], BLOCK, axis=0)
            visit_parts.append(attend(query_rows, key_cache[positions], value_cache[positions], key_factor, value_factor))
        peaks = jnp.stack([entry[0] for entry in visit_parts])
        top_peak = jnp.max(peaks, axis=0)
        factor = jnp.exp(peaks - top_peak)
        denominator = jnp.sum(factor * jnp.stack([entry[1] for entry in visit_parts]), axis=0)
        numerator = jnp.sum(factor[..., None] * jnp.stack([entry[2] for entry in visit_parts]), axis=0)
        attended = (numerator / denominator[..., None]).astype(jnp.bfloat16)
        return attended.reshape(QBLK, HEADS * HEAD_DIM)

    attended = lax.map(one_block, jnp.arange(shards, dtype=jnp.int32)).reshape(QUERIES, HEADS * HEAD_DIM)
    return jnp.dot(attended, out_weight, preferred_element_type=jnp.float32).astype(jnp.bfloat16)
```

```python
import functools
import math

import jax
import jax.numpy as jnp
from jax import lax
from jax.experimental import pallas as pl
from jax.experimental.pallas import tpu as pltpu
from jax.sharding import PartitionSpec as P

BLOCK = 128
STOPS = 6
GLOBAL = 4
NEGATIVE = -1e30
UNROLL = 4
CHUNKS = 8
MESH = pl.DeviceIdType.MESH
VMEM_LIMIT = 60 * 1024 * 1024


def peer(index):
    return {"ctx": index}


def greet(peers, axis="ctx"):
    barrier = pltpu.get_barrier_semaphore()
    for other in peers:
        pl.semaphore_signal(barrier, inc=1, device_id={axis: other}, device_id_type=MESH)
    return barrier


def remote(src, dst, send_sem, recv_sem, device):
    return pltpu.make_async_remote_copy(
        src_ref=src, dst_ref=dst, send_sem=send_sem, recv_sem=recv_sem,
        device_id=device, device_id_type=MESH)


def spread_block(n, me, src, buf, send_sem, recv_sem):
    first = {}
    order = [r for r in range(2, n, 2)]
    for r in order + [1]:
        first[r] = remote(src, buf.at[me], send_sem.at[r], recv_sem.at[r], peer(me ^ r))
        first[r].start()
    for r in order:
        first[r].wait_recv()
        onward = remote(buf.at[me ^ r], buf.at[me ^ r], send_sem.at[r + 1], recv_sem.at[r + 1], peer(me ^ 1))
        onward.start()
        first[r + 1] = onward
    return first


def finish_spread(n, me, buf, first, send_sem, recv_sem):
    order = [r for r in range(2, n, 2)]
    first[1].wait_recv()
    for r in order:
        first[r + 1].wait_recv()
    for r in range(1, n):
        first[r].wait_send()


def gather_kernel(n, q_ref, all_ref, send_sem, recv_sem, local_sem):
    me = lax.axis_index("ctx")
    barrier = greet([me ^ 1] + [me ^ r for r in range(2, n, 2)])
    own = pltpu.make_async_copy(q_ref, all_ref.at[me], local_sem)
    own.start()
    pl.semaphore_wait(barrier, n // 2)
    first = spread_block(n, me, q_ref, all_ref, send_sem, recv_sem)
    finish_spread(n, me, all_ref, first, send_sem, recv_sem)
    own.wait()


def attend_kernel(n, owned, listed, rows, depth,
                  visits, lists, kscale, vscale, q_ref, k_ref, v_ref,
                  part_ref, stat_ref, kraw, vraw, kmask, vmask, score, sems):
    me = lax.axis_index("ctx")
    per = owned // CHUNKS
    span = per * 2 * BLOCK

    def chunk(c, which):
        src, dst = ((k_ref, kraw), (v_ref, vraw))[which]
        where = pl.ds(pl.multiple_of(c * span, span), span)
        return pltpu.make_async_copy(src.at[where], dst.at[where], sems.at[which, c])

    for which in range(2):
        for c in range(CHUNKS):
            chunk(c, which).start()
    row = lax.broadcasted_iota(jnp.int32, (2 * BLOCK, depth), 0)
    odd = (row & 1).astype(jnp.float32)
    odd_b = odd.astype(jnp.bfloat16)
    even_b = (1.0 - odd).astype(jnp.bfloat16)
    for which in range(2):
        raw, masked = ((kraw, kmask), (vraw, vmask))[which]
        for c in range(CHUNKS):
            chunk(c, which).wait()

            @pl.loop(0, per)
            def _(i):
                where = pl.ds(pl.multiple_of((c * per + i) * 2 * BLOCK, 2 * BLOCK), 2 * BLOCK)
                x = raw[where, :]
                masked[where, :depth] = x * even_b
                masked[where, depth:] = x * odd_b

    half = rows // 2
    lane = lax.broadcasted_iota(jnp.int32, (half, BLOCK), 1)
    even_lane = (lane & 1) == 0
    lane2 = lax.broadcasted_iota(jnp.int32, (1, 2 * BLOCK), 1)
    even_lane2 = (lane2 & 1) == 0
    steps = listed // UNROLL
    unit = depth ** -0.5 / math.log(2.0)

    def block_id(b, s, t, u):
        inside = lists[b, s, jnp.minimum(t * UNROLL + u, listed - 1)]
        return jnp.where(t < steps, inside, (t - steps) * UNROLL + u)

    @pl.loop(0, n)
    def _(b):
        s_b = jnp.int32(0)
        has = jnp.int32(0)
        for s in range(STOPS):
            hit = visits[s, b] == me
            s_b = jnp.where(hit, s, s_b)
            has = jnp.where(hit, 1, has)
        t0 = jnp.where(has == 1, 0, steps)
        t1 = jnp.where(me == 0, steps + GLOBAL // UNROLL, steps)
        q4 = q_ref[b].reshape(rows // 32, 2, 16, depth)
        qcat = jnp.concatenate([q4[:, 0].reshape(half, depth), q4[:, 1].reshape(half, depth)], axis=1)

        def first_pass(t, m):
            for u in range(UNROLL):
                blk = block_id(b, s_b, t, u)
                where = pl.ds(pl.multiple_of(blk * 2 * BLOCK, 2 * BLOCK), 2 * BLOCK)
                sc = lax.dot_general(qcat, kmask[where, :], (((1,), (1,)), ((), ())),
                                     preferred_element_type=jnp.float32)
                fac = jnp.where(even_lane2, kscale[blk, 0] * unit, kscale[blk, 1] * unit)
                sc = sc * fac
                score[t, :, u * 2 * BLOCK:(u + 1) * 2 * BLOCK] = sc
                m = jnp.maximum(m, jnp.maximum(sc[:, :BLOCK], sc[:, BLOCK:]))
            return m

        m = lax.fori_loop(t0, t1, first_pass, jnp.full((half, BLOCK), NEGATIVE, jnp.float32))
        p0 = jnp.max(jnp.where(even_lane, m, NEGATIVE), axis=1, keepdims=True)
        p1 = jnp.max(jnp.where(even_lane, NEGATIVE, m), axis=1, keepdims=True)
        pk = jnp.where(even_lane, p0, p1)
        pk2 = jnp.concatenate([pk, pk], axis=1)

        def second_pass(t, carry):
            tot, acc = carry
            ws, vs = [], []
            for u in range(UNROLL):
                blk = block_id(b, s_b, t, u)
                where = pl.ds(pl.multiple_of(blk * 2 * BLOCK, 2 * BLOCK), 2 * BLOCK)
                e = jnp.exp2(score[t, :, u * 2 * BLOCK:(u + 1) * 2 * BLOCK] - pk2)
                tot = tot + (e[:, :BLOCK] + e[:, BLOCK:])
                fac = jnp.where(even_lane2, vscale[blk, 0], vscale[blk, 1])
                ws.append((e * fac).astype(jnp.bfloat16))
                vs.append(vmask[where, :])
            acc = acc + jnp.dot(jnp.concatenate(ws, axis=1), jnp.concatenate(vs, axis=0),
                                preferred_element_type=jnp.float32)
            return tot, acc

        tot, acc = lax.fori_loop(t0, t1, second_pass,
                                 (jnp.zeros((half, BLOCK), jnp.float32),
                                  jnp.zeros((half, 2 * depth), jnp.float32)))
        l0 = jnp.sum(jnp.where(even_lane, tot, 0.0), axis=1, keepdims=True)
        l1 = jnp.sum(jnp.where(even_lane, 0.0, tot), axis=1, keepdims=True)
        table = jnp.where(lane == 0, p0, jnp.where(lane == 1, p1, jnp.where(lane == 2, l0, l1)))
        stat_ref[b] = table.T[:8]
        out = acc.astype(jnp.bfloat16)
        for g in range(2):
            piece = out[:, g * depth:(g + 1) * depth].reshape(rows // 32, 16, depth)
            for qi in range(rows // 32):
                part_ref[b, qi * 32 + g * 16:qi * 32 + g * 16 + 16, :] = piece[qi]


def finish_kernel(n, rows, depth, qblk,
                  part_ref, stat_ref, w_ref, out_ref,
                  wbuf, rpart, rstat, natural, att, gathered, partial, incoming,
                  send_p, recv_p, send_s, recv_s, send_g, recv_g, wsem, local_sem, head_send, head_recv):
    me = lax.axis_index("ctx")
    hd = lax.axis_index("head")
    features, cols = w_ref.shape
    kchunk = features // CHUNKS

    def wcopy(c):
        where = pl.ds(c * kchunk, kchunk)
        return pltpu.make_async_copy(w_ref.at[where], wbuf.at[where], wsem.at[c])

    barrier = greet([me ^ r for r in range(1, n)])
    pl.semaphore_signal(barrier, inc=1, device_id={"head": 1 - hd}, device_id_type=MESH)
    own_p = pltpu.make_async_copy(part_ref.at[me], rpart.at[me], local_sem.at[0])
    own_s = pltpu.make_async_copy(stat_ref.at[me], rstat.at[me], local_sem.at[1])
    own_p.start()
    own_s.start()
    pl.semaphore_wait(barrier, n)
    moves = []
    for r in reversed(range(1, n)):
        to = me ^ r
        a = remote(stat_ref.at[to], rstat.at[me], send_s.at[r], recv_s.at[r], peer(to))
        b = remote(part_ref.at[to], rpart.at[me], send_p.at[r], recv_p.at[r], peer(to))
        a.start()
        b.start()
        moves += [a, b]
    for c in range(CHUNKS):
        wcopy(c).start()
    own_p.wait()
    own_s.wait()
    for m in moves:
        m.wait_recv()
    half = rows // 2
    coefs = []
    for g in range(2):
        p = rstat[:, g, :]
        l = rstat[:, 2 + g, :]
        top = jnp.max(p, axis=0, keepdims=True)
        f = jnp.exp2(p - top)
        den = jnp.sum(f * l, axis=0, keepdims=True)
        coefs.append(f / den)
    for g in range(2):
        cg = coefs[g]
        if n < half:
            cg = jnp.concatenate([cg, jnp.zeros((half - n, half), jnp.float32)], axis=0)
        ct = cg.T
        total = jnp.zeros((half, depth), jnp.float32)
        for slot in range(n):
            w = rpart[slot].reshape(rows // 32, 2, 16, depth)[:, g].reshape(half, depth)
            total = total + ct[:, slot:slot + 1] * w.astype(jnp.float32)
        piece = total.reshape(rows // 32, 16, depth)
        for qi in range(rows // 32):
            natural[qi * 32 + g * 16:qi * 32 + g * 16 + 16, :] = piece[qi]
    for h in range(32):
        att[:, h * depth:(h + 1) * depth] = natural[pl.ds(h, qblk, stride=32), :].astype(jnp.bfloat16)
    own = pltpu.make_async_copy(att, gathered.at[me], local_sem.at[2])
    own.start()
    first = spread_block(n, me, att, gathered, send_g, recv_g)
    finish_spread(n, me, gathered, first, send_g, recv_g)
    own.wait()
    for m in moves:
        m.wait_send()
    for c in range(CHUNKS):
        wcopy(c).wait()
    lhs = gathered[...].astype(jnp.float32).reshape(n * qblk, features).astype(jnp.bfloat16)
    gathered_rows = n * qblk
    mine = gathered_rows // 2
    tile = 512
    outs = []
    for j in range(cols // tile):
        at = slice(j * tile, (j + 1) * tile)
        partial[:, at] = jnp.dot(lhs, wbuf[:, at], preferred_element_type=jnp.float32)
        swap = remote(partial.at[pl.ds(pl.multiple_of((1 - hd) * mine, mine), mine), pl.ds(j * tile, tile)],
                      incoming.at[:, pl.ds(j * tile, tile)],
                      head_send.at[j], head_recv.at[j], {"head": 1 - hd})
        swap.start()
        outs.append(swap)
    for j, swap in enumerate(outs):
        swap.wait_recv()
        at = slice(j * tile, (j + 1) * tile)
        keep = partial[pl.ds(pl.multiple_of(hd * mine, mine), mine), at]
        out_ref[:, at] = (keep + incoming[:, at]).astype(jnp.bfloat16)
    for swap in outs:
        swap.wait_send()


def body(queries, key_cache, value_cache, key_scale, value_scale, visits, key_lists, out_weight):
    n = lax.axis_size("ctx")
    me = lax.axis_index("ctx")
    qblk, heads, depth = queries.shape
    rows = qblk * heads
    positions, kv_local, _ = key_cache.shape
    owned = positions // BLOCK
    listed = key_lists.shape[2]
    features, cols = out_weight.shape
    vm = pl.BlockSpec(memory_space=pltpu.VMEM)
    sm = pl.BlockSpec(memory_space=pltpu.SMEM)
    anyspace = pl.BlockSpec(memory_space=pl.ANY)
    dma = pltpu.SemaphoreType.DMA

    every = pl.pallas_call(
        functools.partial(gather_kernel, n),
        out_shape=jax.ShapeDtypeStruct((n, rows, depth), queries.dtype),
        in_specs=[vm], out_specs=vm,
        scratch_shapes=[dma((n,)), dma((n,)), dma],
        compiler_params=pltpu.CompilerParams(collective_id=0, has_side_effects=True, vmem_limit_bytes=VMEM_LIMIT),
        name="gather_queries",
    )(queries.reshape(rows, depth))

    kscale = lax.dynamic_slice_in_dim(key_scale, me * owned, owned, 0)
    vscale = lax.dynamic_slice_in_dim(value_scale, me * owned, owned, 0)
    parts, stats = pl.pallas_call(
        functools.partial(attend_kernel, n, owned, listed, rows, depth),
        out_shape=(jax.ShapeDtypeStruct((n, rows, depth), jnp.bfloat16),
                   jax.ShapeDtypeStruct((n, 8, BLOCK), jnp.float32)),
        in_specs=[sm, sm, sm, sm, vm, anyspace, anyspace],
        out_specs=(vm, vm),
        scratch_shapes=[
            pltpu.VMEM((positions * kv_local, depth), jnp.bfloat16),
            pltpu.VMEM((positions * kv_local, depth), jnp.bfloat16),
            pltpu.VMEM((positions * kv_local, 2 * depth), jnp.bfloat16),
            pltpu.VMEM((positions * kv_local, 2 * depth), jnp.bfloat16),
            pltpu.VMEM(((listed + GLOBAL) // UNROLL, rows // 2, UNROLL * 2 * BLOCK), jnp.float32),
            dma((2, CHUNKS)),
        ],
        compiler_params=pltpu.CompilerParams(vmem_limit_bytes=VMEM_LIMIT),
        name="attend",
    )(visits, key_lists, kscale, vscale, every,
      key_cache.reshape(positions * kv_local, depth), value_cache.reshape(positions * kv_local, depth))

    return pl.pallas_call(
        functools.partial(finish_kernel, n, rows, depth, qblk),
        out_shape=jax.ShapeDtypeStruct((n * qblk // 2, cols), jnp.bfloat16),
        in_specs=[anyspace, anyspace, anyspace],
        out_specs=vm,
        scratch_shapes=[
            pltpu.VMEM((features, cols), jnp.bfloat16),
            pltpu.VMEM((n, rows, depth), jnp.bfloat16),
            pltpu.VMEM((n, 8, BLOCK), jnp.float32),
            pltpu.VMEM((rows, depth), jnp.float32),
            pltpu.VMEM((qblk, features), jnp.bfloat16),
            pltpu.VMEM((n, qblk, features), jnp.bfloat16),
            pltpu.VMEM((n * qblk, cols), jnp.float32),
            pltpu.VMEM((n * qblk // 2, cols), jnp.float32),
            dma((n,)), dma((n,)), dma((n,)), dma((n,)), dma((n,)), dma((n,)),
            dma((CHUNKS,)), dma((3,)), dma((8,)), dma((8,)),
        ],
        compiler_params=pltpu.CompilerParams(collective_id=1, has_side_effects=True, vmem_limit_bytes=VMEM_LIMIT),
        name="finish",
    )(parts, stats, out_weight)


def solution(mesh):
    return jax.shard_map(
        body,
        mesh=mesh,
        in_specs=(
            P(("groups", "ctx"), "head", None),
            P(("groups", "ctx"), "head", None),
            P(("groups", "ctx"), "head", None),
            P("groups", "head"),
            P("groups", "head"),
            P("groups", None),
            P("groups", None, None),
            P("head", "ctx"),
        ),
        out_specs=P(("groups", "head"), "ctx"),
        check_vma=False,
    )
```

```python
import functools
import math

import jax
import jax.numpy as jnp
from jax import lax
from jax.experimental import pallas as pl
from jax.experimental.pallas import tpu as pltpu
from jax.sharding import PartitionSpec as P

BLOCK = 128
STOPS = 6
GLOBAL = 4
NEGATIVE = -1e30
UNROLL = 4
CHUNKS = 8
MESH = pl.DeviceIdType.MESH
VMEM_LIMIT = 60 * 1024 * 1024


def peer(index):
    return {"ctx": index}


def greet(peers, axis="ctx"):
    barrier = pltpu.get_barrier_semaphore()
    for other in peers:
        pl.semaphore_signal(barrier, inc=1, device_id={axis: other}, device_id_type=MESH)
    return barrier


def remote(src, dst, send_sem, recv_sem, device):
    return pltpu.make_async_remote_copy(
        src_ref=src, dst_ref=dst, send_sem=send_sem, recv_sem=recv_sem,
        device_id=device, device_id_type=MESH)


def spread_block(n, me, src, buf, send_sem, recv_sem):
    first = {}
    order = [r for r in range(2, n, 2)]
    for r in order + [1]:
        first[r] = remote(src, buf.at[me], send_sem.at[r], recv_sem.at[r], peer(me ^ r))
        first[r].start()
    for r in order:
        first[r].wait_recv()
        onward = remote(buf.at[me ^ r], buf.at[me ^ r], send_sem.at[r + 1], recv_sem.at[r + 1], peer(me ^ 1))
        onward.start()
        first[r + 1] = onward
    return first


def finish_spread(n, me, buf, first, send_sem, recv_sem):
    order = [r for r in range(2, n, 2)]
    first[1].wait_recv()
    for r in order:
        first[r + 1].wait_recv()
    for r in range(1, n):
        first[r].wait_send()


def gather_kernel(n, q_ref, all_ref, send_sem, recv_sem, local_sem):
    me = lax.axis_index("ctx")
    barrier = greet([me ^ 1] + [me ^ r for r in range(2, n, 2)])
    own = pltpu.make_async_copy(q_ref, all_ref.at[me], local_sem)
    own.start()
    pl.semaphore_wait(barrier, n // 2)
    first = spread_block(n, me, q_ref, all_ref, send_sem, recv_sem)
    finish_spread(n, me, all_ref, first, send_sem, recv_sem)
    own.wait()


def attend_kernel(n, owned, listed, rows, depth,
                  visits, lists, kscale, vscale, q_ref, k_ref, v_ref,
                  part_ref, stat_ref, kraw, vraw, kmask, vmask, score, sems):
    me = lax.axis_index("ctx")
    base = me * owned
    per = owned // CHUNKS
    span = per * 2 * BLOCK

    def chunk(c, which):
        src, dst = ((k_ref, kraw), (v_ref, vraw))[which]
        where = pl.ds(pl.multiple_of(c * span, span), span)
        return pltpu.make_async_copy(src.at[where], dst.at[where], sems.at[which, c])

    for which in range(2):
        for c in range(CHUNKS):
            chunk(c, which).start()
    row = lax.broadcasted_iota(jnp.int32, (2 * BLOCK, depth), 0)
    odd = (row & 1).astype(jnp.float32)
    odd_b = odd.astype(jnp.bfloat16)
    even_b = (1.0 - odd).astype(jnp.bfloat16)
    for which in range(2):
        raw, masked = ((kraw, kmask), (vraw, vmask))[which]
        for c in range(CHUNKS):
            chunk(c, which).wait()

            @pl.loop(0, per)
            def _(i):
                where = pl.ds(pl.multiple_of((c * per + i) * 2 * BLOCK, 2 * BLOCK), 2 * BLOCK)
                x = raw[where, :]
                masked[where, :depth] = x * even_b
                masked[where, depth:] = x * odd_b

    half = rows // 2
    lane = lax.broadcasted_iota(jnp.int32, (half, BLOCK), 1)
    even_lane = (lane & 1) == 0
    lane2 = lax.broadcasted_iota(jnp.int32, (1, 2 * BLOCK), 1)
    even_lane2 = (lane2 & 1) == 0
    steps = listed // UNROLL
    unit = depth ** -0.5 / math.log(2.0)

    def block_id(b, s, t, u):
        inside = lists[s, b, jnp.minimum(t * UNROLL + u, listed - 1)]
        return jnp.where(t < steps, inside, (t - steps) * UNROLL + u)

    @pl.loop(0, n)
    def _(b):
        s_b = jnp.int32(0)
        has = jnp.int32(0)
        for s in range(STOPS):
            hit = visits[s, b] == me
            s_b = jnp.where(hit, s, s_b)
            has = jnp.where(hit, 1, has)
        t0 = jnp.where(has == 1, 0, steps)
        t1 = jnp.where(me == 0, steps + GLOBAL // UNROLL, steps)
        q4 = q_ref[b].reshape(rows // 32, 2, 16, depth)
        qcat = jnp.concatenate([q4[:, 0].reshape(half, depth), q4[:, 1].reshape(half, depth)], axis=1)

        def first_pass(t, m):
            for u in range(UNROLL):
                blk = block_id(b, s_b, t, u)
                where = pl.ds(pl.multiple_of(blk * 2 * BLOCK, 2 * BLOCK), 2 * BLOCK)
                sc = lax.dot_general(qcat, kmask[where, :], (((1,), (1,)), ((), ())),
                                     preferred_element_type=jnp.float32)
                fac = jnp.where(even_lane2, kscale[0, base + blk] * unit, kscale[1, base + blk] * unit)
                sc = sc * fac
                score[t, :, u * 2 * BLOCK:(u + 1) * 2 * BLOCK] = sc
                m = jnp.maximum(m, jnp.maximum(sc[:, :BLOCK], sc[:, BLOCK:]))
            return m

        m = lax.fori_loop(t0, t1, first_pass, jnp.full((half, BLOCK), NEGATIVE, jnp.float32))
        p0 = jnp.max(jnp.where(even_lane, m, NEGATIVE), axis=1, keepdims=True)
        p1 = jnp.max(jnp.where(even_lane, NEGATIVE, m), axis=1, keepdims=True)
        pk = jnp.where(even_lane, p0, p1)
        pk2 = jnp.concatenate([pk, pk], axis=1)

        def second_pass(t, carry):
            tot, acc = carry
            ws, vs = [], []
            for u in range(UNROLL):
                blk = block_id(b, s_b, t, u)
                where = pl.ds(pl.multiple_of(blk * 2 * BLOCK, 2 * BLOCK), 2 * BLOCK)
                e = jnp.exp2(score[t, :, u * 2 * BLOCK:(u + 1) * 2 * BLOCK] - pk2)
                tot = tot + (e[:, :BLOCK] + e[:, BLOCK:])
                fac = jnp.where(even_lane2, vscale[0, base + blk], vscale[1, base + blk])
                ws.append((e * fac).astype(jnp.bfloat16))
                vs.append(vmask[where, :])
            acc = acc + jnp.dot(jnp.concatenate(ws, axis=1), jnp.concatenate(vs, axis=0),
                                preferred_element_type=jnp.float32)
            return tot, acc

        tot, acc = lax.fori_loop(t0, t1, second_pass,
                                 (jnp.zeros((half, BLOCK), jnp.float32),
                                  jnp.zeros((half, 2 * depth), jnp.float32)))
        l0 = jnp.sum(jnp.where(even_lane, tot, 0.0), axis=1, keepdims=True)
        l1 = jnp.sum(jnp.where(even_lane, 0.0, tot), axis=1, keepdims=True)
        table = jnp.where(lane == 0, p0, jnp.where(lane == 1, p1, jnp.where(lane == 2, l0, l1)))
        stat_ref[b] = table.T[:8]
        out = acc.astype(jnp.bfloat16)
        for g in range(2):
            piece = out[:, g * depth:(g + 1) * depth].reshape(rows // 32, 16, depth)
            for qi in range(rows // 32):
                part_ref[b, qi * 32 + g * 16:qi * 32 + g * 16 + 16, :] = piece[qi]


def finish_kernel(n, rows, depth, qblk,
                  part_ref, stat_ref, w_ref, out_ref,
                  wbuf, rpart, rstat, natural, att, gathered, partial, incoming,
                  send_p, recv_p, send_s, recv_s, send_g, recv_g, wsem, local_sem, head_send, head_recv):
    me = lax.axis_index("ctx")
    hd = lax.axis_index("head")
    features, cols = w_ref.shape
    kchunk = features // CHUNKS

    def wcopy(c):
        where = pl.ds(c * kchunk, kchunk)
        return pltpu.make_async_copy(w_ref.at[where], wbuf.at[where], wsem.at[c])

    barrier = greet([me ^ r for r in range(1, n)])
    pl.semaphore_signal(barrier, inc=1, device_id={"head": 1 - hd}, device_id_type=MESH)
    own_p = pltpu.make_async_copy(part_ref.at[me], rpart.at[me], local_sem.at[0])
    own_s = pltpu.make_async_copy(stat_ref.at[me], rstat.at[me], local_sem.at[1])
    own_p.start()
    own_s.start()
    pl.semaphore_wait(barrier, n)
    moves = []
    for r in reversed(range(1, n)):
        to = me ^ r
        a = remote(stat_ref.at[to], rstat.at[me], send_s.at[r], recv_s.at[r], peer(to))
        b = remote(part_ref.at[to], rpart.at[me], send_p.at[r], recv_p.at[r], peer(to))
        a.start()
        b.start()
        moves += [a, b]
    for c in range(CHUNKS):
        wcopy(c).start()
    own_p.wait()
    own_s.wait()
    for m in moves:
        m.wait_recv()
    half = rows // 2
    coefs = []
    for g in range(2):
        p = rstat[:, g, :]
        l = rstat[:, 2 + g, :]
        top = jnp.max(p, axis=0, keepdims=True)
        f = jnp.exp2(p - top)
        den = jnp.sum(f * l, axis=0, keepdims=True)
        coefs.append(f / den)
    for g in range(2):
        cg = coefs[g]
        if n < half:
            cg = jnp.concatenate([cg, jnp.zeros((half - n, half), jnp.float32)], axis=0)
        ct = cg.T
        total = jnp.zeros((half, depth), jnp.float32)
        for slot in range(n):
            w = rpart[slot].reshape(rows // 32, 2, 16, depth)[:, g].reshape(half, depth)
            total = total + ct[:, slot:slot + 1] * w.astype(jnp.float32)
        piece = total.reshape(rows // 32, 16, depth)
        for qi in range(rows // 32):
            natural[qi * 32 + g * 16:qi * 32 + g * 16 + 16, :] = piece[qi]
    for h in range(32):
        att[:, h * depth:(h + 1) * depth] = natural[pl.ds(h, qblk, stride=32), :].astype(jnp.bfloat16)
    own = pltpu.make_async_copy(att, gathered.at[me], local_sem.at[2])
    own.start()
    first = spread_block(n, me, att, gathered, send_g, recv_g)
    finish_spread(n, me, gathered, first, send_g, recv_g)
    own.wait()
    for m in moves:
        m.wait_send()
    for c in range(CHUNKS):
        wcopy(c).wait()
    lhs = gathered[...].astype(jnp.float32).reshape(n * qblk, features).astype(jnp.bfloat16)
    gathered_rows = n * qblk
    mine = gathered_rows // 2
    tile = 512
    outs = []
    for j in range(cols // tile):
        at = slice(j * tile, (j + 1) * tile)
        partial[:, at] = jnp.dot(lhs, wbuf[:, at], preferred_element_type=jnp.float32)
        swap = remote(partial.at[pl.ds(pl.multiple_of((1 - hd) * mine, mine), mine), pl.ds(j * tile, tile)],
                      incoming.at[:, pl.ds(j * tile, tile)],
                      head_send.at[j], head_recv.at[j], {"head": 1 - hd})
        swap.start()
        outs.append(swap)
    for j, swap in enumerate(outs):
        swap.wait_recv()
        at = slice(j * tile, (j + 1) * tile)
        keep = partial[pl.ds(pl.multiple_of(hd * mine, mine), mine), at]
        out_ref[:, at] = (keep + incoming[:, at]).astype(jnp.bfloat16)
    for swap in outs:
        swap.wait_send()


def body(queries, key_cache, value_cache, key_scale, value_scale, visits, key_lists, out_weight):
    n = lax.axis_size("ctx")
    qblk, heads, depth = queries.shape
    rows = qblk * heads
    positions, kv_local, _ = key_cache.shape
    owned = positions // BLOCK
    listed = key_lists.shape[2]
    features, cols = out_weight.shape
    vm = pl.BlockSpec(memory_space=pltpu.VMEM)
    sm = pl.BlockSpec(memory_space=pltpu.SMEM)
    anyspace = pl.BlockSpec(memory_space=pl.ANY)
    dma = pltpu.SemaphoreType.DMA

    every = pl.pallas_call(
        functools.partial(gather_kernel, n),
        out_shape=jax.ShapeDtypeStruct((n, rows, depth), queries.dtype),
        in_specs=[vm], out_specs=vm,
        scratch_shapes=[dma((n,)), dma((n,)), dma],
        compiler_params=pltpu.CompilerParams(collective_id=0, has_side_effects=True, vmem_limit_bytes=VMEM_LIMIT),
        name="gather_queries",
    )(queries.reshape(rows, depth))

    parts, stats = pl.pallas_call(
        functools.partial(attend_kernel, n, owned, listed, rows, depth),
        out_shape=(jax.ShapeDtypeStruct((n, rows, depth), jnp.bfloat16),
                   jax.ShapeDtypeStruct((n, 8, BLOCK), jnp.float32)),
        in_specs=[sm, sm, sm, sm, vm, anyspace, anyspace],
        out_specs=(vm, vm),
        scratch_shapes=[
            pltpu.VMEM((positions * kv_local, depth), jnp.bfloat16),
            pltpu.VMEM((positions * kv_local, depth), jnp.bfloat16),
            pltpu.VMEM((positions * kv_local, 2 * depth), jnp.bfloat16),
            pltpu.VMEM((positions * kv_local, 2 * depth), jnp.bfloat16),
            pltpu.VMEM(((listed + GLOBAL) // UNROLL, rows // 2, UNROLL * 2 * BLOCK), jnp.float32),
            dma((2, CHUNKS)),
        ],
        compiler_params=pltpu.CompilerParams(vmem_limit_bytes=VMEM_LIMIT),
        name="attend",
    )(visits, jnp.transpose(key_lists, (1, 0, 2)), key_scale.T, value_scale.T, every,
      key_cache.reshape(positions * kv_local, depth), value_cache.reshape(positions * kv_local, depth))

    return pl.pallas_call(
        functools.partial(finish_kernel, n, rows, depth, qblk),
        out_shape=jax.ShapeDtypeStruct((n * qblk // 2, cols), jnp.bfloat16),
        in_specs=[anyspace, anyspace, anyspace],
        out_specs=vm,
        scratch_shapes=[
            pltpu.VMEM((features, cols), jnp.bfloat16),
            pltpu.VMEM((n, rows, depth), jnp.bfloat16),
            pltpu.VMEM((n, 8, BLOCK), jnp.float32),
            pltpu.VMEM((rows, depth), jnp.float32),
            pltpu.VMEM((qblk, features), jnp.bfloat16),
            pltpu.VMEM((n, qblk, features), jnp.bfloat16),
            pltpu.VMEM((n * qblk, cols), jnp.float32),
            pltpu.VMEM((n * qblk // 2, cols), jnp.float32),
            dma((n,)), dma((n,)), dma((n,)), dma((n,)), dma((n,)), dma((n,)),
            dma((CHUNKS,)), dma((3,)), dma((8,)), dma((8,)),
        ],
        compiler_params=pltpu.CompilerParams(collective_id=1, has_side_effects=True, vmem_limit_bytes=VMEM_LIMIT),
        name="finish",
    )(parts, stats, out_weight)


def solution(mesh):
    return jax.shard_map(
        body,
        mesh=mesh,
        in_specs=(
            P(("groups", "ctx"), "head", None),
            P(("groups", "ctx"), "head", None),
            P(("groups", "ctx"), "head", None),
            P("groups", "head"),
            P("groups", "head"),
            P("groups", None),
            P("groups", None, None),
            P("head", "ctx"),
        ),
        out_specs=P(("groups", "head"), "ctx"),
        check_vma=False,
    )
```

```python
import functools
import math

import jax
import jax.numpy as jnp
from jax import lax
from jax.experimental import pallas as pl
from jax.experimental.pallas import tpu as pltpu
from jax.sharding import PartitionSpec as P

BLOCK = 128
STOPS = 6
GLOBAL = 4
NEGATIVE = -1e30
UNROLL = 4
CHUNKS = 8
MESH = pl.DeviceIdType.MESH
VMEM_LIMIT = 67043328


def peer(index):
    return {"ctx": index}


def greet(peers, axis="ctx"):
    barrier = pltpu.get_barrier_semaphore()
    for other in peers:
        pl.semaphore_signal(barrier, inc=1, device_id={axis: other}, device_id_type=MESH)
    return barrier


def remote(src, dst, send_sem, recv_sem, device):
    return pltpu.make_async_remote_copy(
        src_ref=src, dst_ref=dst, send_sem=send_sem, recv_sem=recv_sem,
        device_id=device, device_id_type=MESH)


def spread_block(n, me, src, buf, send_sem, recv_sem):
    first = {}
    order = [r for r in range(2, n, 2)]
    for r in order + [1]:
        first[r] = remote(src, buf.at[me], send_sem.at[r], recv_sem.at[r], peer(me ^ r))
        first[r].start()
    for r in order:
        first[r].wait_recv()
        onward = remote(buf.at[me ^ r], buf.at[me ^ r], send_sem.at[r + 1], recv_sem.at[r + 1], peer(me ^ 1))
        onward.start()
        first[r + 1] = onward
    return first


def finish_spread(n, me, buf, first, send_sem, recv_sem):
    order = [r for r in range(2, n, 2)]
    first[1].wait_recv()
    for r in order:
        first[r + 1].wait_recv()
    for r in range(1, n):
        first[r].wait_send()


def fused_kernel(n, owned, listed, rows, depth, qblk,
                 visits, lists, kscale, vscale, q_ref, k_ref, v_ref, w_ref, out_ref,
                 allq, kraw, vraw, kmask, vmask, score, stage, stab, gstage, gtab, sends,
                 wbuf, rpart, rstat, natural, att, gathered, partial, incoming,
                 ksem, send_q, recv_q, send_p, recv_p, send_s, recv_s, send_g, recv_g,
                 wsem, local_sem, head_send, head_recv):
    me = lax.axis_index("ctx")
    hd = lax.axis_index("head")
    features, cols = w_ref.shape
    kchunk = features // CHUNKS
    base = me * owned
    per = owned // CHUNKS
    span = per * 2 * BLOCK
    half = rows // 2
    sendp = allq
    evens = [r for r in range(2, n, 2)]

    def chunk(c, which):
        src, dst = ((k_ref, kraw), (v_ref, vraw))[which]
        where = pl.ds(c * span, span)
        return pltpu.make_async_copy(src.at[where], dst.at[where], ksem.at[which, c])

    def wcopy(c):
        where = pl.ds(c * kchunk, kchunk)
        return pltpu.make_async_copy(w_ref.at[where], wbuf.at[where], wsem.at[c])

    for which in range(2):
        for c in range(CHUNKS):
            chunk(c, which).start()
    barrier = greet([me ^ r for r in range(1, n)])
    pl.semaphore_signal(barrier, inc=1, device_id={"head": 1 - hd}, device_id_type=MESH)
    own_q = pltpu.make_async_copy(q_ref, allq.at[me], local_sem.at[3])
    own_q.start()
    pl.semaphore_wait(barrier, n)
    first = {}
    for r in evens + [1]:
        first[r] = remote(q_ref, allq.at[me], send_q.at[r], recv_q.at[r], peer(me ^ r))
        first[r].start()

    row = lax.broadcasted_iota(jnp.int32, (2 * BLOCK, depth), 0)
    odd = (row & 1).astype(jnp.float32)
    odd_b = odd.astype(jnp.bfloat16)
    even_b = (1.0 - odd).astype(jnp.bfloat16)

    def mask(which):
        raw, masked = ((kraw, kmask), (vraw, vmask))[which]
        for c in range(CHUNKS):
            chunk(c, which).wait()

        @pl.loop(0, owned)
        def _(i):
            where = pl.ds(pl.multiple_of(i * 2 * BLOCK, 2 * BLOCK), 2 * BLOCK)
            x = raw[where, :]
            masked[i, :, :depth] = x * even_b
            masked[i, :, depth:] = x * odd_b

    mask(0)
    for r in evens:
        first[r].wait_recv()
        first[r + 1] = remote(allq.at[me ^ r], allq.at[me ^ r], send_q.at[r + 1], recv_q.at[r + 1], peer(me ^ 1))
        first[r + 1].start()
    mask(1)
    for c in range(CHUNKS):
        wcopy(c).start()
    own_q.wait()
    finish_spread(n, me, allq, first, send_q, recv_q)

    lane = lax.broadcasted_iota(jnp.int32, (half, BLOCK), 1)
    even_lane = (lane & 1) == 0
    lane2 = lax.broadcasted_iota(jnp.int32, (1, 2 * BLOCK), 1)
    even_lane2 = (lane2 & 1) == 0
    steps = listed // UNROLL
    unit = depth ** -0.5 / math.log(2.0)

    def visit(b, block_id, count, acc_ref, tab_ref):
        q4 = allq[b].reshape(qblk, 2, 16, depth)
        qcat = jnp.concatenate([q4[:, 0].reshape(half, depth), q4[:, 1].reshape(half, depth)], axis=1)

        def first_pass(t, m):
            for u in range(UNROLL):
                blk = block_id(t, u)
                sc = lax.dot_general(qcat, kmask[blk], (((1,), (1,)), ((), ())),
                                     preferred_element_type=jnp.float32)
                fac = jnp.where(even_lane2, kscale[0, base + blk] * unit, kscale[1, base + blk] * unit)
                sc = sc * fac
                score[t, :, u * 2 * BLOCK:(u + 1) * 2 * BLOCK] = sc
                m = jnp.maximum(m, jnp.maximum(sc[:, :BLOCK], sc[:, BLOCK:]))
            return m

        m = lax.fori_loop(0, count, first_pass, jnp.full((half, BLOCK), NEGATIVE, jnp.float32))
        p0 = jnp.max(jnp.where(even_lane, m, NEGATIVE), axis=1, keepdims=True)
        p1 = jnp.max(jnp.where(even_lane, NEGATIVE, m), axis=1, keepdims=True)
        pk = jnp.where(even_lane, p0, p1)
        pk2 = jnp.concatenate([pk, pk], axis=1)

        def second_pass(t, carry):
            tot, acc = carry
            ws, vs = [], []
            for u in range(UNROLL):
                blk = block_id(t, u)
                e = jnp.exp2(score[t, :, u * 2 * BLOCK:(u + 1) * 2 * BLOCK] - pk2)
                tot = tot + (e[:, :BLOCK] + e[:, BLOCK:])
                fac = jnp.where(even_lane2, vscale[0, base + blk], vscale[1, base + blk])
                ws.append((e * fac).astype(jnp.bfloat16))
                vs.append(vmask[blk])
            acc = acc + jnp.dot(jnp.concatenate(ws, axis=1), jnp.concatenate(vs, axis=0),
                                preferred_element_type=jnp.float32)
            return tot, acc

        tot, acc = lax.fori_loop(0, count, second_pass,
                                 (jnp.zeros((half, BLOCK), jnp.float32),
                                  jnp.zeros((half, 2 * depth), jnp.float32)))
        l0 = jnp.sum(jnp.where(even_lane, tot, 0.0), axis=1, keepdims=True)
        l1 = jnp.sum(jnp.where(even_lane, 0.0, tot), axis=1, keepdims=True)
        acc_ref[...] = acc
        tab_ref[...] = jnp.where(lane == 0, p0, jnp.where(lane == 1, p1, jnp.where(lane == 2, l0, l1)))

    @pl.when(me == 0)
    def _():
        @pl.loop(0, n)
        def _(b):
            visit(b, lambda t, u: t * UNROLL + u, GLOBAL // UNROLL, gstage.at[b], gtab.at[b])

    @pl.loop(0, STOPS)
    def _(s):
        b = visits[s, me]
        visit(b, lambda t, u: lists[s, b, t * UNROLL + u], steps, stage.at[s], stab.at[s])

    @pl.loop(0, n)
    def _(r):
        to = me ^ r
        s_b = jnp.int32(0)
        has = jnp.int32(0)
        for s in range(STOPS):
            hit = 1 - jnp.minimum(jnp.abs(visits[s, to] - me), 1)
            s_b = s_b + hit * s
            has = has + hit
        s_b = jnp.minimum(s_b, STOPS - 1)
        keep = has.astype(jnp.float32)
        tab = stab[s_b] * keep + jnp.where(lane < 2, NEGATIVE, 0.0) * (1.0 - keep)
        x = stage[s_b] * keep
        acc = [x[:, g * depth:(g + 1) * depth] for g in range(2)]

        def put(tab, acc):
            sends[r] = tab.T[:8]
            for g in range(2):
                piece = acc[g].astype(jnp.bfloat16).reshape(qblk, 16, depth)
                for qi in range(qblk):
                    sendp[r, qi * 32 + g * 16:qi * 32 + g * 16 + 16, :] = piece[qi]

        @pl.when(me != 0)
        def _():
            put(tab, acc)

        @pl.when(me == 0)
        def _():
            other = gtab[to]
            y = gstage[to]
            mp, ml, ma = [], [], []
            for g in range(2):
                pa, pb = tab[:, g:g + 1], other[:, g:g + 1]
                top = jnp.maximum(pa, pb)
                fa, fb = jnp.exp2(pa - top), jnp.exp2(pb - top)
                mp.append(top)
                ml.append(fa * tab[:, 2 + g:3 + g] + fb * other[:, 2 + g:3 + g])
                ma.append(fa * acc[g] + fb * y[:, g * depth:(g + 1) * depth])
            put(jnp.where(lane == 0, mp[0], jnp.where(lane == 1, mp[1], jnp.where(lane == 2, ml[0], ml[1]))), ma)

    own_p = pltpu.make_async_copy(sendp.at[0], rpart.at[me], local_sem.at[0])
    own_s = pltpu.make_async_copy(sends.at[0], rstat.at[me], local_sem.at[1])
    moves = []
    for r in reversed(range(1, n)):
        to = me ^ r
        a = remote(sends.at[r], rstat.at[me], send_s.at[r], recv_s.at[r], peer(to))
        b = remote(sendp.at[r], rpart.at[me], send_p.at[r], recv_p.at[r], peer(to))
        a.start()
        b.start()
        moves += [a, b]
    own_p.start()
    own_s.start()
    own_p.wait()
    own_s.wait()
    for m in moves:
        m.wait_recv()
    coefs = []
    for g in range(2):
        p = rstat[:, g, :]
        l = rstat[:, 2 + g, :]
        top = jnp.max(p, axis=0, keepdims=True)
        f = jnp.exp2(p - top)
        den = jnp.sum(f * l, axis=0, keepdims=True)
        coefs.append(f / den)
    for g in range(2):
        cg = coefs[g]
        if n < half:
            cg = jnp.concatenate([cg, jnp.zeros((half - n, half), jnp.float32)], axis=0)
        ct = cg.T
        total = jnp.zeros((half, depth), jnp.float32)
        for slot in range(n):
            w = rpart[slot].reshape(rows // 32, 2, 16, depth)[:, g].reshape(half, depth)
            total = total + ct[:, slot:slot + 1] * w.astype(jnp.float32)
        piece = total.reshape(rows // 32, 16, depth)
        for qi in range(rows // 32):
            natural[qi * 32 + g * 16:qi * 32 + g * 16 + 16, :] = piece[qi]
    for h in range(32):
        att[:, h * depth:(h + 1) * depth] = natural[pl.ds(h, qblk, stride=32), :].astype(jnp.bfloat16)
    own = pltpu.make_async_copy(att, gathered.at[me], local_sem.at[2])
    own.start()
    first = spread_block(n, me, att, gathered, send_g, recv_g)
    finish_spread(n, me, gathered, first, send_g, recv_g)
    own.wait()
    for m in moves:
        m.wait_send()
    for c in range(CHUNKS):
        wcopy(c).wait()
    lhs = gathered[...].astype(jnp.float32).reshape(n * qblk, features).astype(jnp.bfloat16)
    gathered_rows = n * qblk
    mine = gathered_rows // 2
    tile = 512
    outs = []
    for j in range(cols // tile):
        at = slice(j * tile, (j + 1) * tile)
        partial[:, at] = jnp.dot(lhs, wbuf[:, at], preferred_element_type=jnp.float32)
        swap = remote(partial.at[pl.ds(pl.multiple_of((1 - hd) * mine, mine), mine), pl.ds(j * tile, tile)],
                      incoming.at[:, pl.ds(j * tile, tile)],
                      head_send.at[j], head_recv.at[j], {"head": 1 - hd})
        swap.start()
        outs.append(swap)
    for j, swap in enumerate(outs):
        swap.wait_recv()
        at = slice(j * tile, (j + 1) * tile)
        keep = partial[pl.ds(pl.multiple_of(hd * mine, mine), mine), at]
        out_ref[:, at] = (keep + incoming[:, at]).astype(jnp.bfloat16)
    for swap in outs:
        swap.wait_send()


def body(queries, key_cache, value_cache, key_scale, value_scale, visits, key_lists, out_weight):
    n = lax.axis_size("ctx")
    qblk, heads, depth = queries.shape
    rows = qblk * heads
    half = rows // 2
    positions, kv_local, _ = key_cache.shape
    owned = positions // BLOCK
    listed = key_lists.shape[2]
    features, cols = out_weight.shape
    vm = pl.BlockSpec(memory_space=pltpu.VMEM)
    sm = pl.BlockSpec(memory_space=pltpu.SMEM)
    anyspace = pl.BlockSpec(memory_space=pl.ANY)
    dma = pltpu.SemaphoreType.DMA
    bf16, f32 = jnp.bfloat16, jnp.float32
    wide = positions * kv_local
    return pl.pallas_call(
        functools.partial(fused_kernel, n, owned, listed, rows, depth, qblk),
        out_shape=jax.ShapeDtypeStruct((n * qblk // 2, cols), bf16),
        in_specs=[sm, sm, sm, sm, vm, anyspace, anyspace, anyspace],
        out_specs=vm,
        scratch_shapes=[
            pltpu.VMEM((n, rows, depth), bf16),
            pltpu.VMEM((wide, depth), bf16),
            pltpu.VMEM((wide, depth), bf16),
            pltpu.VMEM((owned, wide // owned, 2 * depth), bf16),
            pltpu.VMEM((owned, wide // owned, 2 * depth), bf16),
            pltpu.VMEM((listed // UNROLL, half, UNROLL * 2 * BLOCK), f32),
            pltpu.VMEM((STOPS, half, 2 * depth), f32),
            pltpu.VMEM((STOPS, half, BLOCK), f32),
            pltpu.VMEM((n, half, 2 * depth), f32),
            pltpu.VMEM((n, half, BLOCK), f32),
            pltpu.VMEM((n, 8, BLOCK), f32),
            pltpu.VMEM((features, cols), bf16),
            pltpu.VMEM((n, rows, depth), bf16),
            pltpu.VMEM((n, 8, BLOCK), f32),
            pltpu.VMEM((rows, depth), f32),
            pltpu.VMEM((qblk, features), bf16),
            pltpu.VMEM((n, qblk, features), bf16),
            pltpu.VMEM((n * qblk, cols), f32),
            pltpu.VMEM((n * qblk // 2, cols), f32),
            dma((2, CHUNKS)),
            dma((n,)), dma((n,)), dma((n,)), dma((n,)), dma((n,)), dma((n,)), dma((n,)), dma((n,)),
            dma((CHUNKS,)), dma((4,)), dma((8,)), dma((8,)),
        ],
        compiler_params=pltpu.CompilerParams(collective_id=0, has_side_effects=True, vmem_limit_bytes=VMEM_LIMIT),
        name="fused",
    )(visits, jnp.transpose(key_lists, (1, 0, 2)), key_scale.T, value_scale.T, queries.reshape(rows, depth),
      key_cache.reshape(wide, depth), value_cache.reshape(wide, depth), out_weight)


def solution(mesh):
    return jax.shard_map(
        body,
        mesh=mesh,
        in_specs=(
            P(("groups", "ctx"), "head", None),
            P(("groups", "ctx"), "head", None),
            P(("groups", "ctx"), "head", None),
            P("groups", "head"),
            P("groups", "head"),
            P("groups", None),
            P("groups", None, None),
            P("head", "ctx"),
        ),
        out_specs=P(("groups", "head"), "ctx"),
        check_vma=False,
    )
```

```python
import functools
import math

import jax
import jax.numpy as jnp
from jax import lax
from jax.experimental import pallas as pl
from jax.experimental.pallas import tpu as pltpu
from jax.sharding import PartitionSpec as P

BLOCK = 128
STOPS = 6
GLOBAL = 4
NEGATIVE = -1e30
UNROLL = 4
CHUNKS = 8
MESH = pl.DeviceIdType.MESH
VMEM_LIMIT = 67043328


def peer(index):
    return {"ctx": index}


def greet(peers, axis="ctx"):
    barrier = pltpu.get_barrier_semaphore()
    for other in peers:
        pl.semaphore_signal(barrier, inc=1, device_id={axis: other}, device_id_type=MESH)
    return barrier


def remote(src, dst, send_sem, recv_sem, device):
    return pltpu.make_async_remote_copy(
        src_ref=src, dst_ref=dst, send_sem=send_sem, recv_sem=recv_sem,
        device_id=device, device_id_type=MESH)


def launch(n, me, src, buf, send_sem, recv_sem, off=0):
    first = {}
    for r in [r for r in range(2, n, 2)] + [1]:
        first[r] = remote(src, buf.at[me], send_sem.at[off + r], recv_sem.at[off + r], peer(me ^ r))
        first[r].start()
    return first


def pass_on(n, me, buf, first, send_sem, recv_sem, off=0):
    for r in range(2, n, 2):
        first[r].wait_recv()
        first[r + 1] = remote(buf.at[me ^ r], buf.at[me ^ r], send_sem.at[off + r + 1], recv_sem.at[off + r + 1],
                              peer(me ^ 1))
        first[r + 1].start()


def arrive(n, first):
    for r in [1] + [r + 1 for r in range(2, n, 2)]:
        first[r].wait_recv()


def sent(n, first):
    for r in range(1, n):
        first[r].wait_send()


def fused_kernel(n, owned, listed, rows, depth, qblk,
                 visits, lists, kscale, vscale, q_ref, k_ref, v_ref, w_ref, out_ref,
                 allq, kraw, vraw, kmask, vmask, score, stage, stab, gstage, gtab, sends,
                 wbuf, rpart, rstat, natural, att, gathered, partial, incoming,
                 ksem, send_q, recv_q, send_p, recv_p, send_s, recv_s, send_g, recv_g,
                 wsem, local_sem, head_send, head_recv):
    me = lax.axis_index("ctx")
    hd = lax.axis_index("head")
    features, cols = w_ref.shape
    kchunk = features // CHUNKS
    base = me * owned
    per = owned // CHUNKS
    span = per * 2 * BLOCK
    half = rows // 2
    sendp = allq

    def chunk(c, which):
        src, dst = ((k_ref, kraw), (v_ref, vraw))[which]
        where = pl.ds(c * span, span)
        return pltpu.make_async_copy(src.at[where], dst.at[where], ksem.at[which, c])

    def wcopy(c):
        where = pl.ds(c * kchunk, kchunk)
        return pltpu.make_async_copy(w_ref.at[where], wbuf.at[where], wsem.at[c])

    for which in range(2):
        for c in range(CHUNKS):
            chunk(c, which).start()
    barrier = greet([me ^ r for r in range(1, n)])
    pl.semaphore_signal(barrier, inc=1, device_id={"head": 1 - hd}, device_id_type=MESH)
    own_q = pltpu.make_async_copy(q_ref, allq.at[me], local_sem.at[3])
    own_q.start()
    pl.semaphore_wait(barrier, n)
    first = launch(n, me, q_ref, allq, send_q, recv_q)

    row = lax.broadcasted_iota(jnp.int32, (2 * BLOCK, depth), 0)
    odd = (row & 1).astype(jnp.float32)
    odd_b = odd.astype(jnp.bfloat16)
    even_b = (1.0 - odd).astype(jnp.bfloat16)

    def mask(which):
        raw, masked = ((kraw, kmask), (vraw, vmask))[which]
        for c in range(CHUNKS):
            chunk(c, which).wait()

        @pl.loop(0, owned)
        def _(i):
            where = pl.ds(pl.multiple_of(i * 2 * BLOCK, 2 * BLOCK), 2 * BLOCK)
            x = raw[where, :]
            masked[i, :, :depth] = x * even_b
            masked[i, :, depth:] = x * odd_b

    mask(0)
    pass_on(n, me, allq, first, send_q, recv_q)
    mask(1)
    for c in range(CHUNKS):
        wcopy(c).start()
    own_q.wait()
    arrive(n, first)
    sent(n, first)

    lane = lax.broadcasted_iota(jnp.int32, (half, BLOCK), 1)
    even_lane = (lane & 1) == 0
    lane2 = lax.broadcasted_iota(jnp.int32, (1, 2 * BLOCK), 1)
    even_lane2 = (lane2 & 1) == 0
    steps = listed // UNROLL
    unit = depth ** -0.5 / math.log(2.0)

    def visit(b, block_id, count, acc_ref, tab_ref):
        q4 = allq[b].reshape(qblk, 2, 16, depth)
        qcat = jnp.concatenate([q4[:, 0].reshape(half, depth), q4[:, 1].reshape(half, depth)], axis=1)

        def first_pass(t, m):
            for u in range(UNROLL):
                blk = block_id(t, u)
                sc = lax.dot_general(qcat, kmask[blk], (((1,), (1,)), ((), ())),
                                     preferred_element_type=jnp.float32)
                fac = jnp.where(even_lane2, kscale[0, base + blk] * unit, kscale[1, base + blk] * unit)
                sc = sc * fac
                score[t, :, u * 2 * BLOCK:(u + 1) * 2 * BLOCK] = sc
                m = jnp.maximum(m, jnp.maximum(sc[:, :BLOCK], sc[:, BLOCK:]))
            return m

        m = lax.fori_loop(0, count, first_pass, jnp.full((half, BLOCK), NEGATIVE, jnp.float32))
        p0 = jnp.max(jnp.where(even_lane, m, NEGATIVE), axis=1, keepdims=True)
        p1 = jnp.max(jnp.where(even_lane, NEGATIVE, m), axis=1, keepdims=True)
        pk = jnp.where(even_lane, p0, p1)
        pk2 = jnp.concatenate([pk, pk], axis=1)

        def second_pass(t, carry):
            tot, acc = carry
            ws, vs = [], []
            for u in range(UNROLL):
                blk = block_id(t, u)
                e = jnp.exp2(score[t, :, u * 2 * BLOCK:(u + 1) * 2 * BLOCK] - pk2)
                tot = tot + (e[:, :BLOCK] + e[:, BLOCK:])
                fac = jnp.where(even_lane2, vscale[0, base + blk], vscale[1, base + blk])
                ws.append((e * fac).astype(jnp.bfloat16))
                vs.append(vmask[blk])
            acc = acc + jnp.dot(jnp.concatenate(ws, axis=1), jnp.concatenate(vs, axis=0),
                                preferred_element_type=jnp.float32)
            return tot, acc

        tot, acc = lax.fori_loop(0, count, second_pass,
                                 (jnp.zeros((half, BLOCK), jnp.float32),
                                  jnp.zeros((half, 2 * depth), jnp.float32)))
        l0 = jnp.sum(jnp.where(even_lane, tot, 0.0), axis=1, keepdims=True)
        l1 = jnp.sum(jnp.where(even_lane, 0.0, tot), axis=1, keepdims=True)
        acc_ref[...] = acc
        tab_ref[...] = jnp.where(lane == 0, p0, jnp.where(lane == 1, p1, jnp.where(lane == 2, l0, l1)))

    @pl.when(me == 0)
    def _():
        @pl.loop(0, n)
        def _(b):
            visit(b, lambda t, u: t * UNROLL + u, GLOBAL // UNROLL, gstage.at[b], gtab.at[b])

    @pl.loop(0, STOPS)
    def _(s):
        b = visits[s, me]
        visit(b, lambda t, u: lists[s, b, t * UNROLL + u], steps, stage.at[s], stab.at[s])

    @pl.loop(0, n)
    def _(r):
        to = me ^ r
        s_b = jnp.int32(0)
        has = jnp.int32(0)
        for s in range(STOPS):
            hit = 1 - jnp.minimum(jnp.abs(visits[s, to] - me), 1)
            s_b = s_b + hit * s
            has = has + hit
        s_b = jnp.minimum(s_b, STOPS - 1)
        keep = has.astype(jnp.float32)
        tab = stab[s_b] * keep + jnp.where(lane < 2, NEGATIVE, 0.0) * (1.0 - keep)
        x = stage[s_b] * keep
        acc = [x[:, g * depth:(g + 1) * depth] for g in range(2)]

        def put(tab, acc):
            sends[r] = tab.T[:8]
            for g in range(2):
                sendp[r, g * half:(g + 1) * half, :] = acc[g].astype(jnp.bfloat16)

        @pl.when(me != 0)
        def _():
            put(tab, acc)

        @pl.when(me == 0)
        def _():
            other = gtab[to]
            y = gstage[to]
            mp, ml, ma = [], [], []
            for g in range(2):
                pa, pb = tab[:, g:g + 1], other[:, g:g + 1]
                top = jnp.maximum(pa, pb)
                fa, fb = jnp.exp2(pa - top), jnp.exp2(pb - top)
                mp.append(top)
                ml.append(fa * tab[:, 2 + g:3 + g] + fb * other[:, 2 + g:3 + g])
                ma.append(fa * acc[g] + fb * y[:, g * depth:(g + 1) * depth])
            put(jnp.where(lane == 0, mp[0], jnp.where(lane == 1, mp[1], jnp.where(lane == 2, ml[0], ml[1]))), ma)

    own_p = pltpu.make_async_copy(sendp.at[0], rpart.at[me], local_sem.at[0])
    own_s = pltpu.make_async_copy(sends.at[0], rstat.at[me], local_sem.at[1])
    stats, moves = [], [[], []]
    for r in reversed(range(1, n)):
        stats.append(remote(sends.at[r], rstat.at[me], send_s.at[r], recv_s.at[r], peer(me ^ r)))
        stats[-1].start()
    for g in range(2):
        where = pl.ds(g * half, half)
        for r in reversed(range(1, n)):
            moves[g].append(remote(sendp.at[r, where], rpart.at[me, where], send_p.at[g * n + r], recv_p.at[g * n + r],
                                   peer(me ^ r)))
            moves[g][-1].start()
    own_p.start()
    own_s.start()
    own_p.wait()
    own_s.wait()
    for m in stats:
        m.wait_recv()
    heads = rows // qblk // 2
    firsts, owns = [], []
    for g in range(2):
        p = rstat[:, g, :]
        top = jnp.max(p, axis=0, keepdims=True)
        f = jnp.exp2(p - top)
        cg = f / jnp.sum(f * rstat[:, 2 + g, :], axis=0, keepdims=True)
        if n < half:
            cg = jnp.concatenate([cg, jnp.zeros((half - n, half), jnp.float32)], axis=0)
        ct = cg.T
        for m in moves[g]:
            m.wait_recv()
        total = jnp.zeros((half, depth), jnp.float32)
        for slot in range(n):
            total = total + ct[:, slot:slot + 1] * rpart[slot, g * half:(g + 1) * half, :].astype(jnp.float32)
        natural[g] = total
        for h in range(heads):
            att[g, :, h * depth:(h + 1) * depth] = natural[g, pl.ds(h, qblk, stride=heads), :].astype(jnp.bfloat16)
        owns.append(pltpu.make_async_copy(att.at[g], gathered.at[g, me], local_sem.at[2 + 2 * g]))
        owns[g].start()
        firsts.append(launch(n, me, att.at[g], gathered.at[g], send_g, recv_g, g * n))
        if g == 1:
            pass_on(n, me, gathered.at[0], firsts[0], send_g, recv_g, 0)
    mine = n * qblk // 2
    part_features = features // 2
    tile = min(512, cols)
    middle = min(1, cols // tile - 1)
    for c in range(CHUNKS):
        wcopy(c).wait()
    outs = []
    for g in range(2):
        arrive(n, firsts[g])
        owns[g].wait()
        lhs = gathered[g].astype(jnp.float32).reshape(n * qblk, part_features).astype(jnp.bfloat16)
        for j in range(cols // tile):
            at = slice(j * tile, (j + 1) * tile)
            term = jnp.dot(lhs, wbuf[g * part_features:(g + 1) * part_features, at],
                           preferred_element_type=jnp.float32)
            if g == 0:
                partial[:, at] = term
                if j == middle:
                    pass_on(n, me, gathered.at[1], firsts[1], send_g, recv_g, n)
                continue
            partial[:, at] = partial[:, at] + term
            swap = remote(partial.at[pl.ds(pl.multiple_of((1 - hd) * mine, mine), mine), pl.ds(j * tile, tile)],
                          incoming.at[:, pl.ds(j * tile, tile)],
                          head_send.at[j], head_recv.at[j], {"head": 1 - hd})
            swap.start()
            outs.append(swap)
    for j, swap in enumerate(outs):
        swap.wait_recv()
        at = slice(j * tile, (j + 1) * tile)
        keep = partial[pl.ds(pl.multiple_of(hd * mine, mine), mine), at]
        out_ref[:, at] = (keep + incoming[:, at]).astype(jnp.bfloat16)
    for m in stats + moves[0] + moves[1] + outs:
        m.wait_send()
    for g in range(2):
        sent(n, firsts[g])


def body(queries, key_cache, value_cache, key_scale, value_scale, visits, key_lists, out_weight):
    n = lax.axis_size("ctx")
    qblk, heads, depth = queries.shape
    rows = qblk * heads
    half = rows // 2
    positions, kv_local, _ = key_cache.shape
    owned = positions // BLOCK
    listed = key_lists.shape[2]
    features, cols = out_weight.shape
    vm = pl.BlockSpec(memory_space=pltpu.VMEM)
    sm = pl.BlockSpec(memory_space=pltpu.SMEM)
    anyspace = pl.BlockSpec(memory_space=pl.ANY)
    dma = pltpu.SemaphoreType.DMA
    bf16, f32 = jnp.bfloat16, jnp.float32
    wide = positions * kv_local
    return pl.pallas_call(
        functools.partial(fused_kernel, n, owned, listed, rows, depth, qblk),
        out_shape=jax.ShapeDtypeStruct((n * qblk // 2, cols), bf16),
        in_specs=[sm, sm, sm, sm, vm, anyspace, anyspace, anyspace],
        out_specs=vm,
        scratch_shapes=[
            pltpu.VMEM((n, rows, depth), bf16),
            pltpu.VMEM((wide, depth), bf16),
            pltpu.VMEM((wide, depth), bf16),
            pltpu.VMEM((owned, wide // owned, 2 * depth), bf16),
            pltpu.VMEM((owned, wide // owned, 2 * depth), bf16),
            pltpu.VMEM((listed // UNROLL, half, UNROLL * 2 * BLOCK), f32),
            pltpu.VMEM((STOPS, half, 2 * depth), f32),
            pltpu.VMEM((STOPS, half, BLOCK), f32),
            pltpu.VMEM((n, half, 2 * depth), f32),
            pltpu.VMEM((n, half, BLOCK), f32),
            pltpu.VMEM((n, 8, BLOCK), f32),
            pltpu.VMEM((features, cols), bf16),
            pltpu.VMEM((n, rows, depth), bf16),
            pltpu.VMEM((n, 8, BLOCK), f32),
            pltpu.VMEM((2, half, depth), f32),
            pltpu.VMEM((2, qblk, features // 2), bf16),
            pltpu.VMEM((2, n, qblk, features // 2), bf16),
            pltpu.VMEM((n * qblk, cols), f32),
            pltpu.VMEM((n * qblk // 2, cols), f32),
            dma((2, CHUNKS)),
            dma((n,)), dma((n,)), dma((2 * n,)), dma((2 * n,)), dma((n,)), dma((n,)), dma((2 * n,)), dma((2 * n,)),
            dma((CHUNKS,)), dma((5,)), dma((8,)), dma((8,)),
        ],
        compiler_params=pltpu.CompilerParams(collective_id=0, has_side_effects=True, vmem_limit_bytes=VMEM_LIMIT),
        name="fused",
    )(visits, jnp.transpose(key_lists, (1, 0, 2)), key_scale.T, value_scale.T, queries.reshape(rows, depth),
      key_cache.reshape(wide, depth), value_cache.reshape(wide, depth), out_weight)


def solution(mesh):
    return jax.shard_map(
        body,
        mesh=mesh,
        in_specs=(
            P(("groups", "ctx"), "head", None),
            P(("groups", "ctx"), "head", None),
            P(("groups", "ctx"), "head", None),
            P("groups", "head"),
            P("groups", "head"),
            P("groups", None),
            P("groups", None, None),
            P("head", "ctx"),
        ),
        out_specs=P(("groups", "head"), "ctx"),
        check_vma=False,
    )
```

```python
import functools
import math

import jax
import jax.numpy as jnp
from jax import lax
from jax.experimental import pallas as pl
from jax.experimental.pallas import tpu as pltpu
from jax.sharding import PartitionSpec as P

BLOCK = 128
STOPS = 6
GLOBAL = 4
NEGATIVE = -1e30
UNROLL = 16
CHUNKS = 8
MESH = pl.DeviceIdType.MESH
VMEM_LIMIT = 67043328


def peer(index):
    return {"ctx": index}


def greet(peers, axis="ctx"):
    barrier = pltpu.get_barrier_semaphore()
    for other in peers:
        pl.semaphore_signal(barrier, inc=1, device_id={axis: other}, device_id_type=MESH)
    return barrier


def remote(src, dst, send_sem, recv_sem, device):
    return pltpu.make_async_remote_copy(
        src_ref=src, dst_ref=dst, send_sem=send_sem, recv_sem=recv_sem,
        device_id=device, device_id_type=MESH)


def launch(n, me, src, buf, send_sem, recv_sem, off=0):
    first = {}
    for r in [r for r in range(2, n, 2)] + [1]:
        first[r] = remote(src, buf.at[me], send_sem.at[off + r], recv_sem.at[off + r], peer(me ^ r))
        first[r].start()
    return first


def pass_on(n, me, buf, first, send_sem, recv_sem, off=0):
    for r in range(2, n, 2):
        first[r].wait_recv()
        first[r + 1] = remote(buf.at[me ^ r], buf.at[me ^ r], send_sem.at[off + r + 1], recv_sem.at[off + r + 1],
                              peer(me ^ 1))
        first[r + 1].start()


def arrive(n, first):
    for r in [1] + [r + 1 for r in range(2, n, 2)]:
        first[r].wait_recv()


def sent(n, first):
    for r in range(1, n):
        first[r].wait_send()


def fused_kernel(n, owned, listed, rows, depth, qblk,
                 visits, lists, kscale, vscale, q_ref, k_ref, v_ref, w_ref, out_ref,
                 allq, kraw, vraw, kmask, vmask, score, stage, stab, gstage, gtab, sends,
                 wbuf, rpart, rstat, natural, att, gathered, partial, incoming,
                 ksem, send_q, recv_q, send_p, recv_p, send_s, recv_s, send_g, recv_g,
                 wsem, local_sem, head_send, head_recv):
    me = lax.axis_index("ctx")
    hd = lax.axis_index("head")
    features, cols = w_ref.shape
    kchunk = features // CHUNKS
    base = me * owned
    per = owned // CHUNKS
    span = per * 2 * BLOCK
    half = rows // 2
    sendp = allq

    def chunk(c, which):
        src, dst = ((k_ref, kraw), (v_ref, vraw))[which]
        where = pl.ds(c * span, span)
        return pltpu.make_async_copy(src.at[where], dst.at[where], ksem.at[which, c])

    def wcopy(c):
        where = pl.ds(c * kchunk, kchunk)
        return pltpu.make_async_copy(w_ref.at[where], wbuf.at[where], wsem.at[c])

    for which in range(2):
        for c in range(CHUNKS):
            chunk(c, which).start()
    barrier = greet([me ^ r for r in range(1, n)])
    pl.semaphore_signal(barrier, inc=1, device_id={"head": 1 - hd}, device_id_type=MESH)
    own_q = pltpu.make_async_copy(q_ref, allq.at[me], local_sem.at[3])
    own_q.start()
    pl.semaphore_wait(barrier, n)
    first = launch(n, me, q_ref, allq, send_q, recv_q)

    row = lax.broadcasted_iota(jnp.int32, (2 * BLOCK, depth), 0)
    odd = (row & 1).astype(jnp.float32)
    odd_b = odd.astype(jnp.bfloat16)
    even_b = (1.0 - odd).astype(jnp.bfloat16)

    def mask(which):
        raw, masked = ((kraw, kmask), (vraw, vmask))[which]
        for c in range(CHUNKS):
            chunk(c, which).wait()

        @pl.loop(0, owned)
        def _(i):
            where = pl.ds(pl.multiple_of(i * 2 * BLOCK, 2 * BLOCK), 2 * BLOCK)
            x = raw[where, :]
            masked[i, :, :depth] = x * even_b
            masked[i, :, depth:] = x * odd_b

    mask(0)
    pass_on(n, me, allq, first, send_q, recv_q)
    mask(1)
    for c in range(CHUNKS):
        wcopy(c).start()
    own_q.wait()
    arrive(n, first)
    sent(n, first)

    lane = lax.broadcasted_iota(jnp.int32, (half, BLOCK), 1)
    even_lane = (lane & 1) == 0
    lane2 = lax.broadcasted_iota(jnp.int32, (1, 2 * BLOCK), 1)
    even_lane2 = (lane2 & 1) == 0
    steps = listed // UNROLL
    unit = depth ** -0.5 / math.log(2.0)

    def visit(b, block_id, unroll, count, acc_ref, tab_ref):
        q4 = allq[b].reshape(qblk, 2, 16, depth)
        qcat = jnp.concatenate([q4[:, 0].reshape(half, depth), q4[:, 1].reshape(half, depth)], axis=1)

        def first_pass(t, m):
            for u in range(unroll):
                blk = block_id(t, u)
                sc = lax.dot_general(qcat, kmask[blk], (((1,), (1,)), ((), ())),
                                     preferred_element_type=jnp.float32)
                fac = jnp.where(even_lane2, kscale[0, base + blk] * unit, kscale[1, base + blk] * unit)
                sc = sc * fac
                score[t, :, u * 2 * BLOCK:(u + 1) * 2 * BLOCK] = sc
                m = jnp.maximum(m, jnp.maximum(sc[:, :BLOCK], sc[:, BLOCK:]))
            return m

        m = lax.fori_loop(0, count, first_pass, jnp.full((half, BLOCK), NEGATIVE, jnp.float32))
        p0 = jnp.max(jnp.where(even_lane, m, NEGATIVE), axis=1, keepdims=True)
        p1 = jnp.max(jnp.where(even_lane, NEGATIVE, m), axis=1, keepdims=True)
        pk = jnp.where(even_lane, p0, p1)
        pk2 = jnp.concatenate([pk, pk], axis=1)

        def second_pass(t, carry):
            tot, acc = carry
            ws, vs = [], []
            for u in range(unroll):
                blk = block_id(t, u)
                e = jnp.exp2(score[t, :, u * 2 * BLOCK:(u + 1) * 2 * BLOCK] - pk2)
                tot = tot + (e[:, :BLOCK] + e[:, BLOCK:])
                fac = jnp.where(even_lane2, vscale[0, base + blk], vscale[1, base + blk])
                ws.append((e * fac).astype(jnp.bfloat16))
                vs.append(vmask[blk])
            acc = acc + jnp.dot(jnp.concatenate(ws, axis=1), jnp.concatenate(vs, axis=0),
                                preferred_element_type=jnp.float32)
            return tot, acc

        tot, acc = lax.fori_loop(0, count, second_pass,
                                 (jnp.zeros((half, BLOCK), jnp.float32),
                                  jnp.zeros((half, 2 * depth), jnp.float32)))
        l0 = jnp.sum(jnp.where(even_lane, tot, 0.0), axis=1, keepdims=True)
        l1 = jnp.sum(jnp.where(even_lane, 0.0, tot), axis=1, keepdims=True)
        acc_ref[...] = acc
        tab_ref[...] = jnp.where(lane == 0, p0, jnp.where(lane == 1, p1, jnp.where(lane == 2, l0, l1)))

    @pl.when(me == 0)
    def _():
        @pl.loop(0, n)
        def _(b):
            visit(b, lambda t, u: u, GLOBAL, 1, gstage.at[b], gtab.at[b])

    @pl.loop(0, STOPS)
    def _(s):
        b = visits[s, me]
        visit(b, lambda t, u: lists[s, b, t * UNROLL + u], UNROLL, steps, stage.at[s], stab.at[s])

    @pl.loop(0, n)
    def _(r):
        to = me ^ r
        s_b = jnp.int32(0)
        has = jnp.int32(0)
        for s in range(STOPS):
            hit = 1 - jnp.minimum(jnp.abs(visits[s, to] - me), 1)
            s_b = s_b + hit * s
            has = has + hit
        s_b = jnp.minimum(s_b, STOPS - 1)
        keep = has.astype(jnp.float32)
        tab = stab[s_b] * keep + jnp.where(lane < 2, NEGATIVE, 0.0) * (1.0 - keep)
        x = stage[s_b] * keep
        acc = [x[:, g * depth:(g + 1) * depth] for g in range(2)]

        def put(tab, acc):
            sends[r] = tab.T[:8]
            for g in range(2):
                sendp[r, g * half:(g + 1) * half, :] = acc[g].astype(jnp.bfloat16)

        @pl.when(me != 0)
        def _():
            put(tab, acc)

        @pl.when(me == 0)
        def _():
            other = gtab[to]
            y = gstage[to]
            mp, ml, ma = [], [], []
            for g in range(2):
                pa, pb = tab[:, g:g + 1], other[:, g:g + 1]
                top = jnp.maximum(pa, pb)
                fa, fb = jnp.exp2(pa - top), jnp.exp2(pb - top)
                mp.append(top)
                ml.append(fa * tab[:, 2 + g:3 + g] + fb * other[:, 2 + g:3 + g])
                ma.append(fa * acc[g] + fb * y[:, g * depth:(g + 1) * depth])
            put(jnp.where(lane == 0, mp[0], jnp.where(lane == 1, mp[1], jnp.where(lane == 2, ml[0], ml[1]))), ma)

    own_p = pltpu.make_async_copy(sendp.at[0], rpart.at[me], local_sem.at[0])
    own_s = pltpu.make_async_copy(sends.at[0], rstat.at[me], local_sem.at[1])
    stats, moves = [], [[], []]
    for r in reversed(range(1, n)):
        stats.append(remote(sends.at[r], rstat.at[me], send_s.at[r], recv_s.at[r], peer(me ^ r)))
        stats[-1].start()
    for g in range(2):
        where = pl.ds(g * half, half)
        for r in reversed(range(1, n)):
            moves[g].append(remote(sendp.at[r, where], rpart.at[me, where], send_p.at[g * n + r], recv_p.at[g * n + r],
                                   peer(me ^ r)))
            moves[g][-1].start()
    own_p.start()
    own_s.start()
    own_p.wait()
    own_s.wait()
    for m in stats:
        m.wait_recv()
    heads = rows // qblk // 2
    firsts, owns = [], []
    for g in range(2):
        p = rstat[:, g, :]
        top = jnp.max(p, axis=0, keepdims=True)
        f = jnp.exp2(p - top)
        cg = f / jnp.sum(f * rstat[:, 2 + g, :], axis=0, keepdims=True)
        if n < half:
            cg = jnp.concatenate([cg, jnp.zeros((half - n, half), jnp.float32)], axis=0)
        ct = cg.T
        for m in moves[g]:
            m.wait_recv()
        total = jnp.zeros((half, depth), jnp.float32)
        for slot in range(n):
            total = total + ct[:, slot:slot + 1] * rpart[slot, g * half:(g + 1) * half, :].astype(jnp.float32)
        natural[g] = total
        for h in range(heads):
            att[g, :, h * depth:(h + 1) * depth] = natural[g, pl.ds(h, qblk, stride=heads), :].astype(jnp.bfloat16)
        owns.append(pltpu.make_async_copy(att.at[g], gathered.at[g, me], local_sem.at[2 + 2 * g]))
        owns[g].start()
        firsts.append(launch(n, me, att.at[g], gathered.at[g], send_g, recv_g, g * n))
        if g == 1:
            pass_on(n, me, gathered.at[0], firsts[0], send_g, recv_g, 0)
    mine = n * qblk // 2
    part_features = features // 2
    tile = min(512, cols)
    middle = min(1, cols // tile - 1)
    for c in range(CHUNKS):
        wcopy(c).wait()
    outs = []
    for g in range(2):
        arrive(n, firsts[g])
        owns[g].wait()
        lhs = gathered[g].astype(jnp.float32).reshape(n * qblk, part_features).astype(jnp.bfloat16)
        for j in range(cols // tile):
            at = slice(j * tile, (j + 1) * tile)
            term = jnp.dot(lhs, wbuf[g * part_features:(g + 1) * part_features, at],
                           preferred_element_type=jnp.float32)
            if g == 0:
                partial[:, at] = term
                if j == middle:
                    pass_on(n, me, gathered.at[1], firsts[1], send_g, recv_g, n)
                continue
            partial[:, at] = partial[:, at] + term
            swap = remote(partial.at[pl.ds(pl.multiple_of((1 - hd) * mine, mine), mine), pl.ds(j * tile, tile)],
                          incoming.at[:, pl.ds(j * tile, tile)],
                          head_send.at[j], head_recv.at[j], {"head": 1 - hd})
            swap.start()
            outs.append(swap)
    for j, swap in enumerate(outs):
        swap.wait_recv()
        at = slice(j * tile, (j + 1) * tile)
        keep = partial[pl.ds(pl.multiple_of(hd * mine, mine), mine), at]
        out_ref[:, at] = (keep + incoming[:, at]).astype(jnp.bfloat16)
    for m in stats + moves[0] + moves[1] + outs:
        m.wait_send()
    for g in range(2):
        sent(n, firsts[g])


def body(queries, key_cache, value_cache, key_scale, value_scale, visits, key_lists, out_weight):
    n = lax.axis_size("ctx")
    qblk, heads, depth = queries.shape
    rows = qblk * heads
    half = rows // 2
    positions, kv_local, _ = key_cache.shape
    owned = positions // BLOCK
    listed = key_lists.shape[2]
    features, cols = out_weight.shape
    vm = pl.BlockSpec(memory_space=pltpu.VMEM)
    sm = pl.BlockSpec(memory_space=pltpu.SMEM)
    anyspace = pl.BlockSpec(memory_space=pl.ANY)
    dma = pltpu.SemaphoreType.DMA
    bf16, f32 = jnp.bfloat16, jnp.float32
    wide = positions * kv_local
    return pl.pallas_call(
        functools.partial(fused_kernel, n, owned, listed, rows, depth, qblk),
        out_shape=jax.ShapeDtypeStruct((n * qblk // 2, cols), bf16),
        in_specs=[sm, sm, sm, sm, vm, anyspace, anyspace, anyspace],
        out_specs=vm,
        scratch_shapes=[
            pltpu.VMEM((n, rows, depth), bf16),
            pltpu.VMEM((wide, depth), bf16),
            pltpu.VMEM((wide, depth), bf16),
            pltpu.VMEM((owned, wide // owned, 2 * depth), bf16),
            pltpu.VMEM((owned, wide // owned, 2 * depth), bf16),
            pltpu.VMEM((listed // UNROLL, half, UNROLL * 2 * BLOCK), f32),
            pltpu.VMEM((STOPS, half, 2 * depth), f32),
            pltpu.VMEM((STOPS, half, BLOCK), f32),
            pltpu.VMEM((n, half, 2 * depth), f32),
            pltpu.VMEM((n, half, BLOCK), f32),
            pltpu.VMEM((n, 8, BLOCK), f32),
            pltpu.VMEM((features, cols), bf16),
            pltpu.VMEM((n, rows, depth), bf16),
            pltpu.VMEM((n, 8, BLOCK), f32),
            pltpu.VMEM((2, half, depth), f32),
            pltpu.VMEM((2, qblk, features // 2), bf16),
            pltpu.VMEM((2, n, qblk, features // 2), bf16),
            pltpu.VMEM((n * qblk, cols), f32),
            pltpu.VMEM((n * qblk // 2, cols), f32),
            dma((2, CHUNKS)),
            dma((n,)), dma((n,)), dma((2 * n,)), dma((2 * n,)), dma((n,)), dma((n,)), dma((2 * n,)), dma((2 * n,)),
            dma((CHUNKS,)), dma((5,)), dma((8,)), dma((8,)),
        ],
        compiler_params=pltpu.CompilerParams(collective_id=0, has_side_effects=True, vmem_limit_bytes=VMEM_LIMIT),
        name="fused",
    )(visits, jnp.transpose(key_lists, (1, 0, 2)), key_scale.T, value_scale.T, queries.reshape(rows, depth),
      key_cache.reshape(wide, depth), value_cache.reshape(wide, depth), out_weight)


def solution(mesh):
    return jax.shard_map(
        body,
        mesh=mesh,
        in_specs=(
            P(("groups", "ctx"), "head", None),
            P(("groups", "ctx"), "head", None),
            P(("groups", "ctx"), "head", None),
            P("groups", "head"),
            P("groups", "head"),
            P("groups", None),
            P("groups", None, None),
            P("head", "ctx"),
        ),
        out_specs=P(("groups", "head"), "ctx"),
        check_vma=False,
    )
```
